32 devices in a mesh: comp: 2 (over y), tile: 16 (over z, x, core).
Axes of the slice: x: 2, y: 2, z: 4, core: 2. Of those that a mesh axis runs over, the one named last changes fastest.
Arguments:
- model_state: float32 [2, 4, 12, 512, 1024], P('comp', None, None, 'tile'), may hold values from -6 to 6
- sea_mask: int32 [2, 512, 1024], P('comp', 'tile'), may hold values 0 or 1
- diffusion: float32 [2, 4], P('comp'), may hold values from 0.02 to 0.24
- vertical_mix: float32 [2, 4, 12, 12], P('comp'), may hold values from -0.4 to 0.4
- export_mix: float32 [2, 16, 4], P('comp'), may hold values from -3 to 3
- import_mix: float32 [2, 4, 16], P('comp'), may hold values from -1.5 to 1.5
- pair_source: int32 [2, 3072], P('comp', 'tile'), may hold values from 0 to 255
- pair_tile: int32 [2, 3072], P('comp', 'tile'), may hold values from 0 to 15, as said below
- pair_block: int32 [2, 3072], P('comp', 'tile'), may hold values from 0 to 255
- pair_count: int32 [2, 16], P('comp', 'tile'), may hold values from 144 to 192, as said below
- pair_weight: bfloat16 [2, 3072, 128, 128], P('comp', 'tile'), may hold values from -0.5 to 0.5
Outputs:
- advanced_state: float32 [2, 4, 12, 512, 1024], P('comp', None, None, 'tile')
The draws below stay inside these ranges and needn't reach their ends.
Inputs may be any that keep to these rules, and one draw needn't show every extreme that they name: `pair_count`: slots at or beyond a tile's count are unused; in each component some tile uses all 192. `pair_tile`: among the used slots of one tile at most 24 name one destination tile; in each component one destination tile is named 24 times by the used slots of every tile.
All inputs are finite; a program needn't handle non-finite values. No bound on the sum of `sea_mask` on one device may be relied on, other than what follows from the above.
Results may differ from the reference program's by a relative error of at most 0.0015.
Values may be sent and summed in bfloat16 or wider, within the bound.
A program may use at most 192 MiB of HBM per device.

```python
import math
import jax
import jax.numpy as jnp
from jax import lax

FIELDS = 4
LEVELS = 12
CHANNELS = 16
BLOCK_CELLS = 128
STEP_COUNT = 2
ROW_CELLS = 1024
PAIR_SLOTS = 192
TILE_COUNT = 16
GRID_ROWS = 512
BLOCKS_TILE = 256
CAPACITY = 24
PAIRS_ALL = 3072


def draw_pair_count(key, part):
    live_least = (3 * PAIR_SLOTS + 3) // 4
    counts = jax.random.randint(jax.random.fold_in(key, 11), (2, TILE_COUNT), live_least, PAIR_SLOTS + 1)
    fullest = jax.random.randint(jax.random.fold_in(key, 12), (2, 1), 0, TILE_COUNT)
    return jnp.where(jnp.arange(TILE_COUNT)[None, :] == fullest, PAIR_SLOTS, counts).astype(jnp.int32)


def draw_pair_tile(key, part):
    live_least = (3 * PAIR_SLOTS + 3) // 4
    homes = jax.random.randint(jax.random.fold_in(key, 21), (2,), 0, TILE_COUNT).astype(jnp.int32)
    list_keys = jax.random.split(jax.random.fold_in(key, 22), 2 * TILE_COUNT)
    pool_tiles = jnp.repeat(jnp.arange(TILE_COUNT - 1, dtype=jnp.int32), CAPACITY)

    def one_list(each_key, home):
        first_key, second_key = jax.random.split(each_key)
        others = jax.random.permutation(first_key, pool_tiles)[:PAIR_SLOTS - CAPACITY]
        others = others + (others >= home).astype(jnp.int32)
        listing = jnp.concatenate([jnp.full((CAPACITY,), home, jnp.int32), others])
        head_part = jax.random.permutation(second_key, listing[:live_least])
        return jnp.concatenate([head_part, listing[live_least:]])
    home_each = jnp.repeat(homes, TILE_COUNT)
    all_lists = jax.vmap(one_list)(list_keys, home_each)
    return all_lists.reshape(2, TILE_COUNT * PAIR_SLOTS).astype(jnp.int32)


def place_ends(result, stream_key, low, high):
    longest = result.shape.index(max(result.shape))
    spots = []
    for shift in (0, 1):
        where = [jax.random.randint(jax.random.fold_in(stream_key, axis), (), 0, length) for axis, length in enumerate(result.shape)]
        where[longest] = (where[longest] + shift) % result.shape[longest]
        spots.append(tuple(where))
    return result.at[spots[0]].set(low).at[spots[1]].set(high)


def level_of(key, dims, cuts, smallest, high):
    def one(axis_at, blocks):
        steps = jax.random.uniform(jax.random.fold_in(jax.random.fold_in(key, 6), axis_at), (blocks,), jnp.float32, smallest / len(cuts), high / len(cuts))
        return jnp.repeat(jnp.exp(steps), dims[axis_at] // blocks).reshape((-1,) + (1,) * (len(dims) - axis_at - 1))

    level = one(*cuts[0])
    for cut in cuts[1:]:
        level = level * one(*cut)
    return level


def noise(own_key, extent, scale, most, cuts=(), kind=jnp.bfloat16):
    drawn = jax.random.normal(own_key, extent, jnp.float32) * scale
    if len(cuts) > 0:
        drawn = level_of(own_key, extent, cuts, -0.22, 0.18) * drawn
    return jnp.clip(drawn, min=-most, max=most).astype(kind)


def setup_inputs(seed: int = 0) -> dict:
    arg_keys = jax.random.split(jax.random.key(seed), 12)
    return {
        "model_state": noise(arg_keys[0], (2, FIELDS, LEVELS, GRID_ROWS, ROW_CELLS), 1.0, 6.0, ((0, 2), (3, 16)), jnp.float32),
        "sea_mask": place_ends((jax.random.randint(arg_keys[1], (2, GRID_ROWS, ROW_CELLS), 0, 10) < 7).astype(jnp.int32), jax.random.fold_in(arg_keys[1], 1), 0, 1),
        "diffusion": jnp.clip(jnp.exp(math.log(0.24) - 2.4849066 * jax.random.uniform(arg_keys[2], (2, FIELDS), jnp.float32) ** level_of(arg_keys[2], (2, FIELDS), ((0, 2),), -0.2, 0.2)), 0.02, 0.24),
        "vertical_mix": noise(arg_keys[3], (2, FIELDS, LEVELS, LEVELS), 0.08, 0.4, ((0, 2),), jnp.float32),
        "export_mix": noise(arg_keys[4], (2, CHANNELS, FIELDS), FIELDS ** -0.5, 3.0, ((0, 2),), jnp.float32),
        "import_mix": noise(arg_keys[5], (2, FIELDS, CHANNELS), CHANNELS ** -0.5, 1.5, ((0, 2),), jnp.float32),
        "pair_source": place_ends(jax.random.randint(arg_keys[6], (2, PAIRS_ALL), 0, BLOCKS_TILE), jax.random.fold_in(arg_keys[6], 1), 0, BLOCKS_TILE - 1).astype(jnp.int32),
        "pair_tile": draw_pair_tile(jax.random.fold_in(arg_keys[11], 71), 0),
        "pair_block": place_ends(jax.random.randint(arg_keys[8], (2, PAIRS_ALL), 0, BLOCKS_TILE), jax.random.fold_in(arg_keys[8], 1), 0, BLOCKS_TILE - 1).astype(jnp.int32),
        "pair_count": draw_pair_count(jax.random.fold_in(arg_keys[11], 71), 0),
        "pair_weight": noise(arg_keys[10], (2, PAIRS_ALL, BLOCK_CELLS, BLOCK_CELLS), BLOCK_CELLS ** -0.5, 0.5, ((0, 2), (1, 16))),
    }


HIGHEST = lax.Precision.HIGHEST


def advance(current, rate_field, mixing_field):
    padded = jnp.pad(current, ((0, 0), (1, 1), (0, 0)))
    laplace = padded[:, 2:, :] + padded[:, :-2, :] + jnp.roll(current, 1, axis=2) + jnp.roll(current, -1, axis=2) - 4.0 * current
    vertical = jnp.einsum("lm,myx->lyx", mixing_field, current, precision=HIGHEST)
    return current + rate_field * laplace + vertical


def stepped_fields(state_part, rates, mixing):
    def one_field(operands):
        current, rate_field, mixing_field = operands
        for sweep in range(STEP_COUNT):
            current = advance(current, rate_field, mixing_field)
        return current

    return lax.map(one_field, (state_part, rates, mixing))


def remap(exports, pair_source, pair_tile, pair_block, pair_count, pair_weight):
    blocks = exports.reshape(CHANNELS, TILE_COUNT * BLOCKS_TILE, BLOCK_CELLS)
    starts = jnp.arange(TILE_COUNT, dtype=jnp.int32)[:, None] * BLOCKS_TILE
    sources = (starts + pair_source.reshape(TILE_COUNT, PAIR_SLOTS)).astype(jnp.int32)
    targets = (pair_tile.reshape(TILE_COUNT, PAIR_SLOTS) * BLOCKS_TILE + pair_block.reshape(TILE_COUNT, PAIR_SLOTS)).astype(jnp.int32)
    is_live = jnp.arange(PAIR_SLOTS, dtype=jnp.int32)[None, :] < pair_count[:, None]
    weights = pair_weight.reshape(TILE_COUNT, PAIR_SLOTS, BLOCK_CELLS, BLOCK_CELLS)

    def tile_terms(operands):
        tile_sources, tile_weights, tile_live = operands
        picked = blocks[:, tile_sources].astype(jnp.float32)
        contrib = jnp.einsum("kpb,pbc->pkc", picked, tile_weights.astype(jnp.float32), precision=HIGHEST)
        contrib = lax.optimization_barrier(contrib.astype(jnp.bfloat16))
        contrib = contrib.astype(jnp.float32)
        return jnp.where(tile_live[:, None, None], contrib, jnp.zeros((), jnp.float32))

    terms = lax.map(tile_terms, (sources, weights, is_live))
    imports = jnp.zeros((TILE_COUNT * BLOCKS_TILE, CHANNELS, BLOCK_CELLS), jnp.float32)
    imports = imports.at[targets.reshape(-1)].add(terms.reshape(-1, CHANNELS, BLOCK_CELLS))
    return imports.transpose(1, 0, 2).reshape(CHANNELS, GRID_ROWS, ROW_CELLS)


def reference(model_state, sea_mask, diffusion, vertical_mix, export_mix, import_mix, pair_source, pair_tile, pair_block, pair_count, pair_weight):
    imports = []
    for component in range(2):
        exports = jnp.einsum("kf,fyx->kyx", export_mix[component], model_state[component, :, 0], precision=HIGHEST).astype(jnp.bfloat16)
        imports.append(remap(exports, pair_source[component], pair_tile[component], pair_block[component], pair_count[component], pair_weight[component]))
    results = []
    for component in range(2):
        stepped = stepped_fields(model_state[component], diffusion[component], vertical_mix[component])
        forcing = jnp.einsum("fk,kyx->fyx", import_mix[component], imports[1 - component], precision=HIGHEST)
        forcing = forcing * sea_mask[component].astype(jnp.float32)
        results.append(stepped.at[:, 0].add(forcing))
    return jnp.stack(results)
```

```python
import functools

import jax
import jax.numpy as jnp
from jax import lax
from jax.experimental import pallas as pl
from jax.experimental.pallas import tpu as pltpu
from jax.sharding import PartitionSpec as P

CELLS = 128
GROUP = 16
LANE = 32
PARTS = 4
HIGHEST = lax.Precision.HIGHEST
MESH = pl.DeviceIdType.MESH
F32 = jnp.float32
BF16 = jnp.bfloat16


def iota(shape, dim):
    return lax.broadcasted_iota(jnp.int32, shape, dim)


def onehot(cond, dtype=F32):
    return jnp.where(cond, 1.0, 0.0).astype(dtype)


def exact_dot(a, b):
    return jnp.dot(a, b, precision=HIGHEST, preferred_element_type=F32)


def split(x):
    high = x.astype(BF16)
    return high, (x - high.astype(F32)).astype(BF16)


def two_step_matrix(lhs_ref, vmix_ref, diff_ref, f, levels):
    side = levels * GROUP
    cols = side + 4 * GROUP
    d = diff_ref[0, f]
    eye = onehot(iota((levels, levels), 0) == iota((levels, levels), 1))
    base = vmix_ref[0, :, f, :] + eye * (1.0 - 4.0 * d)
    twice = exact_dot(base, base) + eye * (4.0 * d * d)
    once = base * (2.0 * d)

    def source_level(shape):
        col = iota(shape, 1)
        return jnp.where(col < side, col // GROUP, (col - side) % GROUP)

    def source_row(shape):
        col = iota(shape, 1)
        edge = (col - side) // GROUP
        edge = jnp.where(edge < 2, edge - 2, edge + GROUP - 2)
        return jnp.where(col < side, col % GROUP, edge)

    right = onehot(iota((levels, cols), 0) == source_level((levels, cols)), BF16)
    left = onehot(iota((side, levels), 0) // GROUP == iota((side, levels), 1), BF16)
    wide = []
    for part in (*split(twice), *split(once)):
        wide.append(jnp.dot(part, right, preferred_element_type=F32).astype(BF16))
    wide = jnp.dot(left, jnp.concatenate(wide, axis=1), preferred_element_type=F32)
    gap = jnp.abs(iota((side, cols), 0) % GROUP - source_row((side, cols)))
    same = iota((side, cols), 0) // GROUP == source_level((side, cols))
    square = jnp.full((side, cols), d * d, F32)
    square_high = square.astype(BF16).astype(F32)
    for part, sq in ((0, square_high), (1, square - square_high)):
        two = wide[:, part * cols : (part + 1) * cols]
        one = wide[:, (2 + part) * cols : (3 + part) * cols]
        sq = jnp.where(same, sq, 0.0)
        p = jnp.where(gap == 0, one, jnp.where(gap == 1, 2.0 * sq, 0.0))
        q = jnp.where(gap == 0, two, jnp.where(gap == 1, one, jnp.where(gap == 2, sq, 0.0)))
        lhs_ref[f, 0:side, part * cols : (part + 1) * cols] = p.astype(BF16)
        lhs_ref[f, side : 2 * side, part * cols : (part + 1) * cols] = q.astype(BF16)


def main_kernel(
    chunk,
    src_ref,
    count_ref,
    diff_ref,
    tile_ref,
    block_ref,
    emix_ref,
    imix_ref,
    vmix_ref,
    state_hbm,
    w_hbm,
    recv_ref,
    ids_ref,
    out_ref,
    st,
    wbuf,
    edge_buf,
    exports,
    contribs,
    mixed,
    payload,
    id_rows,
    place,
    im_send,
    im_recv,
    edges,
    halo,
    meta,
    lhs_ref,
    xs0,
    xs1,
    pq0,
    pq1,
    edge_sem,
    top_sem,
    w_sem,
    st_sem,
    pay_send_sem,
    pay_recv_sem,
    id_send_sem,
    id_recv_sem,
    small_send_sem,
    small_recv_sem,
):
    me_c = lax.axis_index("comp")
    me_t = lax.axis_index("tile")
    n = recv_ref.shape[0]
    other = 1 - me_c
    above = lax.rem(me_t + 1, n)
    below = lax.rem(me_t + n - 1, n)
    fields, levels, rows, width = st.shape
    channels = emix_ref.shape[2]
    xblocks = width // CELLS
    slots = wbuf.shape[0]
    per = slots // PARTS
    side = levels * GROUP
    wide = mixed.shape[0]

    def edge_copies(f):
        return (
            pltpu.make_async_copy(
                state_hbm.at[0, f, :, 0:8, :], edge_buf.at[0, f], edge_sem.at[0, f]
            ),
            pltpu.make_async_copy(
                state_hbm.at[0, f, :, rows - 8 : rows, :], edge_buf.at[1, f], edge_sem.at[1, f]
            ),
        )

    def top_copy(f):
        return pltpu.make_async_copy(state_hbm.at[0, f, 0], st.at[f, 0], top_sem.at[f])

    def w_copy(i):
        at = pl.ds(i * per, per)
        return pltpu.make_async_copy(w_hbm.at[0, at], wbuf.at[at], w_sem.at[i])

    def st_copy(f):
        at = pl.ds(1, levels - 1)
        return pltpu.make_async_copy(state_hbm.at[0, f, at], st.at[f, at], st_sem.at[f])

    def halo_copies():
        return (
            pltpu.make_async_remote_copy(
                src_ref=edges.at[0],
                dst_ref=halo.at[1],
                send_sem=small_send_sem.at[0],
                recv_sem=small_recv_sem.at[0],
                device_id=(me_c, below),
                device_id_type=MESH,
            ),
            pltpu.make_async_remote_copy(
                src_ref=edges.at[1],
                dst_ref=halo.at[0],
                send_sem=small_send_sem.at[1],
                recv_sem=small_recv_sem.at[1],
                device_id=(me_c, above),
                device_id_type=MESH,
            ),
        )

    def mix_copy():
        return pltpu.make_async_remote_copy(
            src_ref=im_send,
            dst_ref=im_recv,
            send_sem=small_send_sem.at[2],
            recv_sem=small_recv_sem.at[2],
            device_id=(other, me_t),
            device_id_type=MESH,
        )

    def id_copy(to, source_slot):
        return pltpu.make_async_remote_copy(
            src_ref=id_rows.at[to],
            dst_ref=ids_ref.at[source_slot],
            send_sem=id_send_sem.at[to],
            recv_sem=id_recv_sem.at[source_slot],
            device_id=(other, to),
            device_id_type=MESH,
        )

    def pay_copy(to, source_slot):
        return pltpu.make_async_remote_copy(
            src_ref=payload.at[to],
            dst_ref=recv_ref.at[source_slot],
            send_sem=pay_send_sem.at[to],
            recv_sem=pay_recv_sem.at[source_slot],
            device_id=(other, to),
            device_id_type=MESH,
        )

    for f in range(fields):
        for copy in edge_copies(f):
            copy.start()
    for f in range(fields):
        top_copy(f).start()
    for i in range(PARTS):
        w_copy(i).start()

    barrier = pltpu.get_barrier_semaphore()

    def greet(t, carry):
        pl.semaphore_signal(barrier, inc=1, device_id=(other, t), device_id_type=MESH)
        return carry

    lax.fori_loop(0, n, greet, 0)
    pl.semaphore_signal(barrier, inc=1, device_id=(me_c, above), device_id_type=MESH)
    pl.semaphore_signal(barrier, inc=1, device_id=(me_c, below), device_id_type=MESH)

    im_send[...] = jnp.zeros_like(im_send)
    im_send[0:fields, 0:channels] = imix_ref[0]

    meta[...] = jnp.zeros_like(meta)
    meta[0:1, 0:slots] = tile_ref[...]
    meta[1:2, 0:slots] = block_ref[...]
    lane = iota((1, wide), 1)
    live = lane < count_ref[0, 0]
    tiles = jnp.where(live, meta[0:1, :], -1)
    square_row = iota((wide, wide), 0)
    square_col = iota((wide, wide), 1)
    tile_square = jnp.broadcast_to(tiles, (wide, wide))
    tile_col = jnp.sum(jnp.where(square_row == square_col, tile_square, 0), axis=1, keepdims=True)
    match = (tile_col == tile_square) & (square_row < square_col)
    rank = jnp.sum(jnp.where(match, 1, 0), axis=0, keepdims=True)
    slot = jnp.where(live, tiles * chunk + rank, -1)
    dest = jnp.where(
        (iota((n, wide), 0) == tiles) & live,
        jnp.broadcast_to(meta[1:2, :] + 1, (n, wide)),
        0,
    )
    base = lax.rem(me_t, CELLS // LANE) * LANE
    spot = onehot(iota((CELLS, wide), 0) == rank + base, BF16)
    index_rows = lax.dot_general(
        dest.astype(F32).astype(BF16), spot, (((1,), (1,)), ((), ())), preferred_element_type=F32
    )
    for t in range(n):
        id_rows[t] = jnp.broadcast_to(index_rows[t : t + 1, :], (8, CELLS)).astype(BF16)
    place[...] = onehot(iota((n * chunk, wide), 0) == slot, BF16)
    mixed[slots:, :] = jnp.zeros((wide - slots, fields * CELLS), BF16)

    edges[...] = jnp.zeros_like(edges)
    for f in range(fields):
        for copy in edge_copies(f):
            copy.wait()
        for r in range(2):
            edges[0, f, r, 0:levels] = edge_buf[0, f, :, r, :].astype(BF16)
            edges[1, f, r, 0:levels] = edge_buf[1, f, :, 6 + r, :].astype(BF16)

    @pl.when(me_t == 0)
    def _():
        for f in range(fields):
            halo[0, f, 0] = (0.0 - edges[0, f, 0].astype(F32)).astype(BF16)
            halo[0, f, 1] = jnp.zeros(halo.shape[3:], BF16)

    @pl.when(me_t == n - 1)
    def _():
        for f in range(fields):
            halo[1, f, 0] = jnp.zeros(halo.shape[3:], BF16)
            halo[1, f, 1] = (0.0 - edges[1, f, 1].astype(F32)).astype(BF16)

    pl.semaphore_wait(barrier, n + 2)
    down, up = halo_copies()

    @pl.when(me_t > 0)
    def _():
        down.start()

    @pl.when(me_t < n - 1)
    def _():
        up.start()

    mix_copy().start()

    def send_ids(k, carry):
        id_copy(lax.rem(me_t + k, n), me_t).start()
        return carry

    lax.fori_loop(0, n, send_ids, 0)

    for f in range(fields):
        two_step_matrix(lhs_ref, vmix_ref, diff_ref, f, levels)

    sub = 8
    erows = sub * channels
    ecols = sub * fields
    left = onehot(iota((erows, channels), 0) % channels == iota((erows, channels), 1))
    right = onehot(iota((fields, 3 * ecols), 0) == iota((fields, 3 * ecols), 1) % ecols // sub)
    spread = lax.dot_general(
        left,
        emix_ref[0],
        (((1,), (1,)), ((), ())),
        precision=HIGHEST,
        preferred_element_type=F32,
    )
    spread = exact_dot(spread, right)
    spread = jnp.where(
        iota((erows, 3 * ecols), 0) // channels == iota((erows, 3 * ecols), 1) % sub, spread, 0.0
    )
    high, low = split(spread)
    part = iota((erows, 3 * ecols), 1) // ecols
    spread = jnp.where(part == 1, low.astype(F32), high.astype(F32)).astype(BF16)
    for f in range(fields):
        top_copy(f).wait()
    for g in range(rows // sub):
        s = st[:, 0, g * sub : (g + 1) * sub, :].reshape(ecols, width)
        sh, sl = split(s)
        e = jnp.dot(spread, jnp.concatenate([sh, sh, sl], axis=0), preferred_element_type=F32)
        e = e.astype(BF16)
        for y in range(sub):
            for xb in range(xblocks):
                exports[(g * sub + y) * xblocks + xb] = e[
                    y * channels : (y + 1) * channels, xb * CELLS : (xb + 1) * CELLS
                ]

    brows = fields * GROUP
    bcols = GROUP * channels
    blend = None
    for i in range(PARTS):
        w_copy(i).wait()
        st_copy(i).start()
        for p in range(i * per, (i + 1) * per):
            c = jnp.dot(exports[src_ref[0, p]], wbuf[p], preferred_element_type=F32)
            at = (p % GROUP) * channels
            contribs[p // GROUP, at : at + channels, :] = c.astype(BF16)
        if i == 0:
            mix_copy().wait()
            left = onehot(iota((brows, 8), 0) // GROUP == iota((brows, 8), 1))
            right = onehot(iota((CELLS, bcols), 0) == iota((CELLS, bcols), 1) % channels)
            blend = exact_dot(exact_dot(left, im_recv[...]), right)
            blend = jnp.where(
                iota((brows, bcols), 0) % GROUP == iota((brows, bcols), 1) // channels, blend, 0.0
            )
            blend = jnp.concatenate(split(blend), axis=0)
        for g in range(i * per // GROUP, (i + 1) * per // GROUP):
            m = jnp.dot(blend, contribs[g], preferred_element_type=F32)
            m = (m[:brows] + m[brows:]).astype(BF16)
            for f in range(fields):
                mixed[g * GROUP : (g + 1) * GROUP, f * CELLS : (f + 1) * CELLS] = m[
                    f * GROUP : (f + 1) * GROUP, :
                ]
    for d in range(0, n, 8):
        block = jnp.dot(
            place[d * chunk : (d + 8) * chunk, :], mixed[...], preferred_element_type=F32
        )
        for j in range(8):
            payload[d + j] = block[j * chunk : (j + 1) * chunk, :].astype(BF16)

    def send(k, carry):
        pay_copy(lax.rem(me_t + k, n), me_t).start()
        return carry

    lax.fori_loop(0, n, send, 0)

    @pl.when(me_t > 0)
    def _():
        down.wait_send()
        up.wait_recv()

    @pl.when(me_t < n - 1)
    def _():
        up.wait_send()
        down.wait_recv()

    cols = side + 4 * GROUP
    for xs in (xs0, xs1):
        xs[side:cols, :] = jnp.zeros((4 * GROUP, width), BF16)
        xs[cols + side :, :] = jnp.zeros((4 * GROUP, width), BF16)

    def prepare(xs, f, g):
        for l in range(levels):
            vh, vl = split(st[f, l, g * GROUP : (g + 1) * GROUP, :])
            xs[l * GROUP : (l + 1) * GROUP] = vh
            xs[cols + l * GROUP : cols + (l + 1) * GROUP] = vl
        for b in range(2):
            outer, inner = (b, b + 2) if g == 0 else (b + 2, b)
            own = GROUP + b if g == 0 else GROUP - 2 + b
            xs[side + outer * GROUP : side + (outer + 1) * GROUP] = halo[g, f, b]
            at = side + inner * GROUP
            xs[at : at + levels] = st[f, :, own, :].astype(BF16)

    def product(xs, pq, f):
        a = lhs_ref[f]
        a = jnp.concatenate([a, a[:, :cols]], axis=1)
        x = jnp.concatenate([xs[0:cols], xs[0:cols], xs[cols : 2 * cols]], axis=0)
        pq[...] = jnp.dot(a, x, preferred_element_type=F32)

    def finish(xs, pq, f, g):
        d = diff_ref[0, f]
        for l in range(levels):
            p = pq[l * GROUP : (l + 1) * GROUP, :]
            q = pq[side + l * GROUP : side + (l + 1) * GROUP, :]
            v = xs[l * GROUP : (l + 1) * GROUP]
            far = (pltpu.roll(v, 2, 1) + pltpu.roll(v, width - 2, 1)).astype(F32)
            out_ref[f, l, g * GROUP : (g + 1) * GROUP, :] = (q + far * (d * d)) + (
                pltpu.roll(p, 1, 1) + pltpu.roll(p, width - 1, 1)
            )

    bufs = ((xs0, pq0), (xs1, pq1))
    pending = None
    for f in range(fields):
        st_copy(f).wait()
        for g in range(2):
            xs, pq = bufs[g]
            prepare(xs, f, g)
            product(xs, pq, f)
            if pending is not None:
                finish(*pending)
            pending = (xs, pq, f, g)
    finish(*pending)

    def drain(t, carry):
        id_copy(t, t).wait()
        pay_copy(t, t).wait()
        return carry

    lax.fori_loop(0, n, drain, 0)


def last_kernel(v_ref, recv_ref, ids_ref, mask_ref, out_hbm, hits, packed, top, body_sem, top_sem):
    fields, levels, rows, width = v_ref.shape
    n, chunk = recv_ref.shape[0], recv_ref.shape[1]
    xblocks = width // CELLS
    per_group = CELLS // LANE

    def body_copy(f):
        at = pl.ds(1, levels - 1)
        return pltpu.make_async_copy(v_ref.at[f, at], out_hbm.at[0, f, at], body_sem.at[f])

    def top_copy(f):
        return pltpu.make_async_copy(top.at[f], out_hbm.at[0, f, 0], top_sem.at[f])

    for f in range(fields):
        body_copy(f).start()
    for g in range(n // per_group):
        ids = jnp.zeros((8, CELLS), F32)
        for j in range(per_group):
            ids = ids + ids_ref[g * per_group + j].astype(F32)
        ids = ids[0:1, :].astype(jnp.int32) - 1
        spot = jnp.where(ids >= 0, (ids % xblocks) * rows + ids // xblocks, -1)
        hits[:, g * CELLS : (g + 1) * CELLS] = onehot(
            iota((rows * xblocks, CELLS), 0) == spot, BF16
        )
    for t in range(n):
        packed[t, 0:chunk, :] = recv_ref[t]
        packed[t, chunk:, :] = jnp.zeros((LANE - chunk, packed.shape[2]), BF16)
    for f in range(fields):
        part = packed[:, :, f * CELLS : (f + 1) * CELLS].reshape(n * LANE, CELLS)
        forcing = jnp.dot(hits[...], part, preferred_element_type=F32)
        for xb in range(xblocks):
            at = slice(xb * CELLS, (xb + 1) * CELLS)
            top[f, :, at] = v_ref[f, 0, :, at] + forcing[
                xb * rows : (xb + 1) * rows, :
            ] * mask_ref[0, :, at].astype(F32)
        top_copy(f).start()
    for f in range(fields):
        top_copy(f).wait()
        body_copy(f).wait()


def local(
    model_state,
    sea_mask,
    diffusion,
    vertical_mix,
    export_mix,
    import_mix,
    pair_source,
    pair_tile,
    pair_block,
    pair_count,
    pair_weight,
):
    _, fields, levels, rows, width = model_state.shape
    channels = export_mix.shape[1]
    n = lax.axis_size("tile")
    slots = pair_source.shape[1]
    cap = (2 * slots + n - 1) // n
    chunk = -(-cap // 8) * 8
    wide = -(-slots // 128) * 128
    blocks = rows * width // CELLS
    side = levels * GROUP
    cols = side + 4 * GROUP

    smem = pl.BlockSpec(memory_space=pltpu.SMEM)
    vmem = pl.BlockSpec(memory_space=pltpu.VMEM)
    hbm = pl.BlockSpec(memory_space=pltpu.HBM)

    received, ids, stepped = pl.pallas_call(
        functools.partial(main_kernel, chunk),
        out_shape=(
            pltpu.VMEM((n, chunk, fields * CELLS), BF16),
            pltpu.VMEM((n, 8, CELLS), BF16),
            pltpu.VMEM((fields, levels, rows, width), F32),
        ),
        in_specs=[smem, smem, smem, vmem, vmem, vmem, vmem, vmem, hbm, hbm],
        out_specs=(vmem, vmem, vmem),
        scratch_shapes=[
            pltpu.VMEM((fields, levels, rows, width), F32),
            pltpu.VMEM((slots, CELLS, CELLS), BF16),
            pltpu.VMEM((2, fields, levels, 8, width), F32),
            pltpu.VMEM((blocks, channels, CELLS), BF16),
            pltpu.VMEM((slots // GROUP, GROUP * channels, CELLS), BF16),
            pltpu.VMEM((wide, fields * CELLS), BF16),
            pltpu.VMEM((n, chunk, fields * CELLS), BF16),
            pltpu.VMEM((n, 8, CELLS), BF16),
            pltpu.VMEM((n * chunk, wide), BF16),
            pltpu.VMEM((8, CELLS), F32),
            pltpu.VMEM((8, CELLS), F32),
            pltpu.VMEM((2, fields, 2, GROUP, width), BF16),
            pltpu.VMEM((2, fields, 2, GROUP, width), BF16),
            pltpu.VMEM((8, wide), jnp.int32),
            pltpu.VMEM((fields, 2 * side, 2 * cols), BF16),
            pltpu.VMEM((2 * cols, width), BF16),
            pltpu.VMEM((2 * cols, width), BF16),
            pltpu.VMEM((2 * side, width), F32),
            pltpu.VMEM((2 * side, width), F32),
            pltpu.SemaphoreType.DMA((2, fields)),
            pltpu.SemaphoreType.DMA((fields,)),
            pltpu.SemaphoreType.DMA((PARTS,)),
            pltpu.SemaphoreType.DMA((fields,)),
            pltpu.SemaphoreType.DMA((n,)),
            pltpu.SemaphoreType.DMA((n,)),
            pltpu.SemaphoreType.DMA((n,)),
            pltpu.SemaphoreType.DMA((n,)),
            pltpu.SemaphoreType.DMA((3,)),
            pltpu.SemaphoreType.DMA((3,)),
        ],
        compiler_params=pltpu.CompilerParams(
            collective_id=0, has_side_effects=True, vmem_limit_bytes=50 << 20
        ),
    )(
        pair_source,
        pair_count,
        diffusion,
        pair_tile,
        pair_block,
        export_mix.transpose(0, 2, 1),
        import_mix,
        vertical_mix.transpose(0, 2, 1, 3),
        model_state,
        pair_weight,
    )

    return pl.pallas_call(
        last_kernel,
        out_shape=jax.ShapeDtypeStruct(model_state.shape, F32),
        in_specs=[vmem, vmem, vmem, vmem],
        out_specs=hbm,
        scratch_shapes=[
            pltpu.VMEM((blocks, n * LANE), BF16),
            pltpu.VMEM((n, LANE, fields * CELLS), BF16),
            pltpu.VMEM((fields, rows, width), F32),
            pltpu.SemaphoreType.DMA((fields,)),
            pltpu.SemaphoreType.DMA((fields,)),
        ],
        compiler_params=pltpu.CompilerParams(vmem_limit_bytes=40 << 20),
    )(stepped, received, ids, sea_mask)


def solution(mesh):
    return jax.shard_map(
        local,
        mesh=mesh,
        in_specs=(
            P("comp", None, None, "tile", None),
            P("comp", "tile", None),
            P("comp", None),
            P("comp", None, None, None),
            P("comp", None, None),
            P("comp", None, None),
            P("comp", "tile"),
            P("comp", "tile"),
            P("comp", "tile"),
            P("comp", "tile"),
            P("comp", "tile", None, None),
        ),
        out_specs=P("comp", None, None, "tile", None),
        check_vma=False,
    )
```
